512 devices in a mesh: sib: 8 (over z_hi, x), leaf: 64 (over y, z_lo, core).
Axes of the slice: x: 4, y: 8, z: 8 (z_hi: 2, z_lo: 4; z = z_hi * 4 + z_lo), core: 2. Of those that a mesh axis runs over, the one named last changes fastest.
Arguments:
- t_int: float32 [64, 512, 1024], P('leaf', 'sib'), as said below
- t_ext: float32 [64, 512, 512], P('leaf', 'sib'), may hold values from -6 to 6
- iface_map: int32 [64, 512], P('leaf'), may hold values from 0 to 511, each once within a row
Outputs:
- own_map: float32 [64, 512, 512], P('leaf', 'sib')
- cross_map: float32 [64, 512, 512], P('leaf', 'sib')
- solution_op: float32 [64, 512, 512], P('leaf', 'sib')
The draws below stay inside these ranges and needn't reach their ends.
Inputs may be any that keep to these rules, and one draw needn't show every extreme that they name: For each box, the last 512 columns of t_int form a symmetric matrix equal to the identity plus a positive semidefinite matrix. `iface_map`: each row is a permutation of 0 to 511.
All inputs are finite; a program needn't handle non-finite values.
Results may differ from the reference program's by a relative error of at most 0.0003.
Values sent between devices are 32-bit elements; how exact they have to be, the bound alone decides.
A program may use at most 64 MiB of HBM per device.

```python
import jax
import jax.numpy as jnp
from jax import lax

NE = 512
NI = 512
BOXES = 64
PAIRS = 32


def draw_t_int(key, part):
    key_cross = jax.random.fold_in(jax.random.fold_in(key, 11), 0)
    key_gram = jax.random.fold_in(jax.random.fold_in(key, 11), 1)
    key_column = jax.random.fold_in(jax.random.fold_in(key, 11), 3)
    column_scale = jnp.exp(jax.random.uniform(key_column, (BOXES, 1, NI), jnp.float32, -3.5, 3.5))
    coupling = 0.25 * jax.random.normal(key_cross, (BOXES, NI, NE), jnp.float32)
    factor = jax.random.normal(key_gram, (BOXES, NI, NI), jnp.float32)
    factor = factor * column_scale
    gram = jnp.einsum('bik,bjk->bij', factor, factor, precision=jax.lax.Precision.HIGHEST) / NI
    gram = 0.5 * (gram + jnp.swapaxes(gram, 1, 2)) + jnp.eye(NI, dtype=jnp.float32)[None]
    return jnp.concatenate([coupling, gram], axis=2).astype(jnp.float32)


def block_scale(key, extent, shards, smallest, largest):
    loudness, own = 1.0, jax.random.fold_in(key, 6)
    for position, shards_of in shards:
        steps = jnp.exp(jax.random.uniform(jax.random.fold_in(own, position), (shards_of,), jnp.float32, smallest / len(shards), largest / len(shards)))
        loudness = loudness * jnp.repeat(steps, extent[position] // shards_of).reshape([-1 if axis == position else 1 for axis in range(len(extent))])
    return loudness


def scatter_about(own_key, shape, width, most, shards=(), kind=jnp.bfloat16):
    level = block_scale(own_key, shape, shards, -0.22, 0.18) if shards else 1.0
    result = jax.random.normal(own_key, shape, jnp.float32) * width * level
    return jnp.minimum(jnp.maximum(result, -most), most).astype(kind)


def setup_inputs(seed: int = 0) -> dict:
    arg_keys = jax.random.split(jax.random.key(seed), 4)
    return {
        "t_int": draw_t_int(jax.random.fold_in(arg_keys[3], 71), 0),
        "t_ext": scatter_about(arg_keys[1], (BOXES, NE, NE), 1.0, 6.0, ((0, 64), (1, 8)), jnp.float32),
        "iface_map": jax.vmap(lambda own: jax.random.permutation(own, NI))(jax.random.split(arg_keys[2], BOXES)).reshape((BOXES, NI)).astype(jnp.int32),
    }


def common_order(matrix, index_map):
    inverse = jnp.zeros((NI,), jnp.int32).at[index_map].set(jnp.arange(NI, dtype=jnp.int32))
    picked = matrix[inverse]
    return (picked[:, :NE], picked[:, NE + inverse])

def lower_solve(factor, right_side, flipped):
    return lax.linalg.triangular_solve(factor, right_side, left_side=True, lower=True, transpose_a=flipped)

def product(left, right):
    return jnp.dot(left.astype(jnp.float32), right.astype(jnp.float32), precision=lax.Precision.HIGHEST, preferred_element_type=jnp.float32)

def merge_pair(inputs):
    first_rows, second_rows, first_ext, second_ext, first_map, second_map = inputs
    outer_a, iface_a = common_order(first_rows, first_map)
    outer_b, iface_b = common_order(second_rows, second_map)
    factor = jnp.linalg.cholesky(iface_a + iface_b)
    solved_a = lower_solve(factor, outer_a, False)
    solved_b = lower_solve(factor, outer_b, False)
    own_a = first_ext - product(solved_a.T, solved_a)
    own_b = second_ext - product(solved_b.T, solved_b)
    cross_a = -product(solved_a.T, solved_b)
    cross_b = -product(solved_b.T, solved_a)
    sol_a = -lower_solve(factor, solved_a, True)
    sol_b = -lower_solve(factor, solved_b, True)
    return (own_a, own_b, cross_a, cross_b, sol_a, sol_b)

def reference(t_int, t_ext, iface_map):
    inputs = (t_int[:PAIRS], t_int[PAIRS:], t_ext[:PAIRS], t_ext[PAIRS:], iface_map[:PAIRS], iface_map[PAIRS:])
    own_a, own_b, cross_a, cross_b, sol_a, sol_b = lax.map(merge_pair, inputs)
    own_map = jnp.concatenate([own_a, own_b], axis=0)
    cross_map = jnp.concatenate([cross_a, cross_b], axis=0)
    solution_op = jnp.concatenate([sol_a, sol_b], axis=0)
    return (own_map, cross_map, solution_op)
```

```python
import jax
import jax.numpy as jnp
from jax import lax
from jax.experimental import pallas as pl
from jax.experimental.pallas import tpu as pltpu
from jax.sharding import PartitionSpec as P

MESH = pl.DeviceIdType.MESH
POINTS = 512
ROWS = 64
HALF = 32
BLOCK = 128
XR, XL, RR, RL, Y, Z, YC, ZC = 0, 8, 16, 20, 24, 26, 28, 29
COPIES = 30


def matmul(a, b, dims=((1,), (0,))):
    return lax.dot_general(a, b, (dims, ((), ())), preferred_element_type=jnp.float32)


def exact_matmul(a, b):
    return jnp.dot(a, b, precision=lax.Precision.HIGHEST, preferred_element_type=jnp.float32)


def thirds(x):
    high = x.astype(jnp.bfloat16)
    rest = x - high.astype(jnp.float32)
    mid = rest.astype(jnp.bfloat16)
    low = (rest - mid.astype(jnp.float32)).astype(jnp.bfloat16)
    return high, mid, low


def halves(x):
    high = x.astype(jnp.bfloat16)
    return high, (x - high.astype(jnp.float32)).astype(jnp.bfloat16)


def select_rows(onehot, x):
    high, mid, low = thirds(x)
    return matmul(onehot, high) + (matmul(onehot, mid) + matmul(onehot, low))


def select_columns(x, onehot, dims):
    high, mid, low = thirds(x)
    return matmul(high, onehot, dims) + (matmul(mid, onehot, dims) + matmul(low, onehot, dims))


def product(a, b):
    a_high, a_low = halves(a)
    b_high, b_low = halves(b)
    return matmul(a_high, b_high) + (matmul(a_high, b_low) + matmul(a_low, b_high))


def block_inverse(strips):
    lane = lax.broadcasted_iota(jnp.int32, (8, BLOCK), 1)
    sub = lax.broadcasted_iota(jnp.int32, (8, BLOCK), 0)
    row_of = lambda x, j: jnp.broadcast_to(x[j : j + 1, :], (8, BLOCK))
    column_of = lambda x, l: jnp.broadcast_to(x[:, l : l + 1], (8, BLOCK))
    strips = list(strips)
    for k in range(len(strips)):
        own = strips[k]
        cols = [column_of(own, 8 * k + j) for j in range(8)]
        pivots = (lane >= 8 * k) & (lane < 8 * k + 8)
        s = jnp.where(pivots, jnp.where(lane - 8 * k == sub, 1.0, 0.0), own)
        for j in range(8):
            here = sub == j
            inverse = 1.0 / row_of(cols[j], j)
            factor = jnp.where(here, -1.0, cols[j])
            for q in range(j + 1, 8):
                t = factor * row_of(cols[q], j)
                cols[q] = jnp.where(here, 0.0, cols[q]) - t * inverse
            s = jnp.where(here, 0.0, s) - (factor * row_of(s, j)) * inverse
        rows = [row_of(s, j) for j in range(8)]
        for i in range(len(strips)):
            if i == k:
                continue
            x = strips[i]
            t = [column_of(x, 8 * k + j) * rows[j] for j in range(8)]
            while len(t) > 1:
                t = [t[a] + t[a + 1] for a in range(0, len(t), 2)]
            strips[i] = jnp.where(pivots, 0.0, x) - t[0]
        strips[k] = s
    return jnp.concatenate(strips, axis=0)


def eliminate(a, panel, k):
    at = pl.ds(k * BLOCK, BLOCK)
    inverse = block_inverse([a[pl.ds(k * BLOCK + 8 * i, 8), at] for i in range(BLOCK // 8)])
    panel[...] = exact_matmul(inverse, a[at, :])
    panel[:, at] = inverse
    a[at, at] = jnp.zeros((BLOCK, BLOCK), jnp.float32)
    column = a[:, at]
    a[:, at] = jnp.zeros((POINTS, BLOCK), jnp.float32)
    a[...] = a[...] - exact_matmul(column, panel[...])
    a[at, :] = panel[...]


class Exchange:
    def __init__(self, own, gathered, send_sem, recv_sem, near):
        self.own, self.gathered, self.near = own, gathered, near
        self.send_sem, self.recv_sem = send_sem, recv_sem
        self.copies = {}

    def slot(self, kind, x, half):
        z = self.near["z"] if kind < 2 else 1 - self.near["z"]
        row = (kind % 2) * POINTS + (z * 4 + x) * ROWS + half * HALF
        return self.gathered.at[pl.ds(row, HALF), :]

    def source(self, kind, half):
        if kind == 0:
            return self.own(half)
        return self.slot(kind, self.near["x"], half)

    def send(self, index, src, dst, to):
        copy = pltpu.make_async_remote_copy(
            src_ref=src, dst_ref=dst, send_sem=self.send_sem.at[index], recv_sem=self.recv_sem.at[index],
            device_id=self.near[to], device_id_type=MESH,
        )
        copy.start()
        self.copies[index] = copy

    def arrived(self, index):
        self.copies[index].wait_recv()

    def along_x(self, kind, half):
        dst = self.slot(kind, self.near["x"], half)
        src = self.source(kind, half)
        self.send(XR + 2 * kind + half, src, dst, "right")
        self.send(XL + 2 * kind + half, src, dst, "left")

    def relay_x(self, kind):
        x = self.near["x"]
        self.arrived(XR + 2 * kind)
        block = self.slot(kind, (x + 3) % 4, 0)
        self.send(RR + kind, block, block, "right")
        self.arrived(XL + 2 * kind + 1)
        block = self.slot(kind, (x + 1) % 4, 1)
        self.send(RL + kind, block, block, "left")

    def first(self):
        for half in (0, 1):
            self.send(Y + half, self.own(half), self.slot(1, self.near["x"], half), "across_y")
            self.send(Z + 1 - half, self.own(1 - half), self.slot(0, self.near["x"], 1 - half), "across_z")
        self.along_x(0, 0)
        self.along_x(0, 1)

    def second(self):
        x = self.near["x"]
        self.arrived(Y)
        block = self.slot(1, x, 0)
        self.send(ZC, block, block, "across_z")
        self.along_x(1, 0)
        self.arrived(Z + 1)
        self.send(YC, self.slot(2, x, 1), self.slot(3, x, 1), "across_y")
        self.along_x(2, 1)
        self.relay_x(0)
        self.arrived(Y + 1)
        self.along_x(1, 1)
        self.arrived(Z)
        self.along_x(2, 0)

    def third(self):
        self.arrived(ZC)
        self.along_x(3, 0)
        self.arrived(YC)
        self.along_x(3, 1)
        self.relay_x(1)
        self.relay_x(2)

    def fourth(self):
        self.relay_x(3)

    def last(self):
        for kind in range(4):
            self.arrived(XR + 2 * kind + 1)
            self.arrived(XL + 2 * kind)
            self.arrived(RR + kind)
            self.arrived(RL + kind)

    def sent(self):
        for copy in self.copies.values():
            copy.wait_send()


def kernel(t_ref, ext_ref, map_ref, own_ref, cross_ref, sol_ref,
           iface, outer, other_map, a, panel, send_sem, recv_sem, map_sem):
    sib, leaf = lax.axis_index("sib"), lax.axis_index("leaf")
    leaves = lax.axis_size("leaf")
    x, z = sib % 4, sib // 4
    near = {
        "x": x, "z": z,
        "right": {"sib": z * 4 + (x + 1) % 4},
        "left": {"sib": z * 4 + (x + 3) % 4},
        "across_z": {"sib": (sib + 4) % 8},
        "across_y": {"leaf": (leaf + leaves // 2) % leaves},
    }
    barrier = pltpu.get_barrier_semaphore()
    for name in ("right", "left", "across_z", "across_y"):
        pl.semaphore_signal(barrier, inc=1, device_id=near[name], device_id_type=MESH)
    pl.semaphore_wait(barrier, 4)

    map_copy = pltpu.make_async_remote_copy(
        src_ref=map_ref, dst_ref=other_map, send_sem=map_sem.at[0], recv_sem=map_sem.at[1],
        device_id=near["across_y"], device_id_type=MESH,
    )
    map_copy.start()
    own_half = lambda column: lambda half: t_ref.at[pl.ds(half * HALF, HALF), pl.ds(column, POINTS)]
    g = Exchange(own_half(POINTS), iface, send_sem.at[0], recv_sem.at[0], near)
    r = Exchange(own_half(0), outer, send_sem.at[1], recv_sem.at[1], near)
    g.first()
    mine = pl.ds(pl.multiple_of(sib * ROWS, ROWS), ROWS)
    iface[mine, :] = t_ref[:, POINTS:]
    outer[mine, :] = t_ref[:, :POINTS]
    g.second()
    map_copy.wait()
    point = lax.broadcasted_iota(jnp.int32, (POINTS, POINTS), 0)
    own_onehot = jnp.where(point == map_ref[...], 1.0, 0.0).astype(jnp.bfloat16)
    other_onehot = jnp.where(point == other_map[...], 1.0, 0.0).astype(jnp.bfloat16)
    shuffle = matmul(own_onehot, other_onehot, ((0,), (0,))).astype(jnp.bfloat16)
    g.third()
    g.fourth()
    r.first()
    g.last()
    permuted = select_columns(iface[pl.ds(POINTS, POINTS), :], shuffle, ((1,), (1,)))
    a[...] = iface[pl.ds(0, POINTS), :] + select_rows(shuffle, permuted)
    for k, step in enumerate((r.second, r.third, r.fourth, r.last)):
        eliminate(a, panel, k)
        step()

    wide = outer[pl.ds(0, POINTS), pl.ds(pl.multiple_of(sib // 2 * BLOCK, BLOCK), BLOCK)]
    wide = pltpu.roll(wide, (sib % 2) * ROWS, 1)[:, :ROWS]
    right = product(wide.T, a[...])
    rows = lax.broadcasted_iota(jnp.int32, (ROWS, POINTS), 0) + sib * ROWS
    chosen = select_rows(jnp.where(rows == map_ref[...], 1.0, 0.0).astype(jnp.bfloat16), a[...])
    both = product(jnp.concatenate([right, chosen], axis=0), outer[pl.ds(0, POINTS), :])
    own_ref[...] = ext_ref[...] - both[:ROWS]
    sol_ref[...] = -both[ROWS:]
    moved = select_columns(right, shuffle, ((1,), (0,)))
    cross_ref[...] = -product(moved, outer[pl.ds(POINTS, POINTS), :])
    g.sent()
    r.sent()


def on_device(t_int, t_ext, iface_map):
    vmem = pl.BlockSpec(memory_space=pltpu.VMEM)
    block = jax.ShapeDtypeStruct((ROWS, POINTS), jnp.float32)
    outs = pl.pallas_call(
        kernel,
        out_shape=(block,) * 3,
        in_specs=[vmem] * 3,
        out_specs=(vmem,) * 3,
        scratch_shapes=[
            pltpu.VMEM((2 * POINTS, POINTS), jnp.float32),
            pltpu.VMEM((2 * POINTS, POINTS), jnp.float32),
            pltpu.VMEM((1, POINTS), jnp.int32),
            pltpu.VMEM((POINTS, POINTS), jnp.float32),
            pltpu.VMEM((BLOCK, POINTS), jnp.float32),
            pltpu.SemaphoreType.DMA((2, COPIES)),
            pltpu.SemaphoreType.DMA((2, COPIES)),
            pltpu.SemaphoreType.DMA((2,)),
        ],
        compiler_params=pltpu.CompilerParams(collective_id=0, has_side_effects=True),
    )(t_int[0], t_ext[0], iface_map)
    return tuple(out[None] for out in outs)


def solution(mesh):
    placed = (P("leaf", "sib", None), P("leaf", "sib", None), P("leaf", None))
    return jax.shard_map(
        on_device,
        mesh=mesh,
        in_specs=placed,
        out_specs=(P("leaf", "sib", None),) * 3,
        check_vma=False,
    )
```

```python
import jax
import jax.numpy as jnp
from jax import lax
from jax.experimental import pallas as pl
from jax.experimental.pallas import tpu as pltpu
from jax.sharding import PartitionSpec as P

MESH = pl.DeviceIdType.MESH
POINTS = 512
ROWS = 64
HALF = 32
BLOCK = 128
PANEL = 2
STRIPS = BLOCK // 8
XR, XL, RR, RL, Y, Z, YC, ZC = 0, 16, 32, 48, 64, 68, 72, 76
COPIES = 80


def matmul(a, b, dims=((1,), (0,))):
    return lax.dot_general(a, b, (dims, ((), ())), preferred_element_type=jnp.float32)


def exact_matmul(a, b):
    return jnp.dot(a, b, precision=lax.Precision.HIGHEST, preferred_element_type=jnp.float32)


def thirds(x):
    high = x.astype(jnp.bfloat16)
    rest = x - high.astype(jnp.float32)
    mid = rest.astype(jnp.bfloat16)
    low = (rest - mid.astype(jnp.float32)).astype(jnp.bfloat16)
    return high, mid, low


def halves(x):
    high = x.astype(jnp.bfloat16)
    return high, (x - high.astype(jnp.float32)).astype(jnp.bfloat16)


def select_rows(onehot, x):
    high, mid, low = thirds(x)
    return matmul(onehot, high) + (matmul(onehot, mid) + matmul(onehot, low))


def select_columns(x, onehot, dims):
    high, mid, low = thirds(x)
    return matmul(high, onehot, dims) + (matmul(mid, onehot, dims) + matmul(low, onehot, dims))


def product(a, b):
    a_high, a_low = halves(a)
    b_high, b_low = halves(b)
    return matmul(a_high, b_high) + (matmul(a_high, b_low) + matmul(a_low, b_high))


def pivot_panel(own, first):
    lane = lax.broadcasted_iota(jnp.int32, (8, BLOCK), 1)
    sub = lax.broadcasted_iota(jnp.int32, (8, BLOCK), 0)
    width = 8 * len(own)
    cols = [[column_of(x, 8 * first + j) for x in own] for j in range(width)]
    pivots = (lane >= 8 * first) & (lane < 8 * first + width)
    s = [jnp.where(pivots, jnp.where(lane - 8 * (first + n) == sub, 1.0, 0.0), x) for n, x in enumerate(own)]
    for j in range(width):
        at, row = divmod(j, 8)
        here = sub == row
        inverse = 1.0 / row_of(cols[j][at], row)
        factor = [jnp.where(here, -1.0, x) if n == at else x for n, x in enumerate(cols[j])]

        def reduced(xs):
            r = row_of(xs[at], row)
            return [(jnp.where(here, 0.0, x) if n == at else x) - (f * r) * inverse for n, (x, f) in enumerate(zip(xs, factor))]

        for q in range(j + 1, width):
            cols[q] = reduced(cols[q])
        s = reduced(s)
    return s, pivots


def row_of(x, j):
    return jnp.broadcast_to(x[j : j + 1, :], (8, BLOCK))


def column_of(x, lane):
    return jnp.broadcast_to(x[:, lane : lane + 1], (8, BLOCK))


def block_inverse(strips):
    strips = list(strips)
    for k in range(0, STRIPS, PANEL):
        s, pivots = pivot_panel(strips[k : k + PANEL], k)
        soon = range(k + PANEL, min(STRIPS, k + 2 * PANEL))
        rest = [i for i in range(STRIPS) if not k <= i < k + PANEL and i not in soon]
        old = list(strips)
        for i in soon:
            t = [column_of(old[i], 8 * k + j) * row_of(s[j // 8], j % 8) for j in range(8 * PANEL)]
            while len(t) > 1:
                t = [t[n] + t[n + 1] for n in range(0, len(t), 2)]
            strips[i] = jnp.where(pivots, 0.0, old[i]) - t[0]
        left = jnp.concatenate([jnp.where(pivots, old[i], 0.0) for i in rest], axis=0)
        zero = jnp.zeros((8, BLOCK), jnp.float32)
        right = jnp.concatenate([s[i - k] if k <= i < k + PANEL else zero for i in range(STRIPS)], axis=0)
        change = exact_matmul(left, right)
        for n, i in enumerate(rest):
            strips[i] = jnp.where(pivots, 0.0, old[i]) - change[8 * n : 8 * n + 8]
        strips[k : k + PANEL] = s
    return jnp.concatenate(strips, axis=0)


def eliminate(a, panel, k):
    at = pl.ds(k * BLOCK, BLOCK)
    inverse = block_inverse([a[pl.ds(k * BLOCK + 8 * i, 8), at] for i in range(BLOCK // 8)])
    panel[...] = exact_matmul(inverse, a[at, :])
    panel[:, at] = inverse
    a[at, at] = jnp.zeros((BLOCK, BLOCK), jnp.float32)
    column = a[:, at]
    a[:, at] = jnp.zeros((POINTS, BLOCK), jnp.float32)
    a[...] = a[...] - exact_matmul(column, panel[...])
    a[at, :] = panel[...]


class Exchange:
    def __init__(self, own, view, send_sem, recv_sem, near, has_more):
        self.own, self.view, self.near, self.has_more = own, view, near, has_more
        self.send_sem, self.recv_sem = send_sem, recv_sem

    def copy(self, index, src, dst, to):
        return pltpu.make_async_remote_copy(
            src_ref=src, dst_ref=dst, send_sem=self.send_sem.at[index], recv_sem=self.recv_sem.at[index],
            device_id=self.near[to], device_id_type=MESH,
        )

    def over_y(self, c):
        return self.copy(Y + c, self.own(c), self.view(1, self.near["x"], c), "across_y")

    def over_z(self, c):
        return self.copy(Z + c, self.own(c), self.view(0, self.near["x"], c), "across_z")

    def corner(self, c):
        x = self.near["x"]
        if c % 2:
            return self.copy(YC + c, self.view(2, x, c), self.view(3, x, c), "across_y")
        return self.copy(ZC + c, self.view(1, x, c), self.view(1, x, c), "across_z")

    def to_right(self, kind, c):
        x = self.near["x"]
        src = self.own(c) if kind == 0 else self.view(kind, x, c)
        return self.copy(XR + 4 * kind + c, src, self.view(kind, x, c), "right")

    def to_left(self, kind, c):
        x = self.near["x"]
        src = self.own(c) if kind == 0 else self.view(kind, x, c)
        return self.copy(XL + 4 * kind + c, src, self.view(kind, x, c), "left")

    def onward(self, kind, c):
        x = self.near["x"]
        if c % 2:
            block = self.view(kind, (x + 1) % 4, c)
            return self.copy(RL + 4 * kind + c, block, block, "left")
        block = self.view(kind, (x + 3) % 4, c)
        return self.copy(RR + 4 * kind + c, block, block, "right")

    def along_x(self, kind, c):
        self.to_right(kind, c).start()
        self.to_left(kind, c).start()

    def relay_x(self, kind, c):
        (self.to_left if c % 2 else self.to_right)(kind, c).wait_recv()
        self.onward(kind, c).start()

    def more(self, kind, run):
        if self.has_more is not None:
            pl.when(self.has_more(kind))(run)

    def first(self):
        def run(even, odd):
            self.over_y(even).start()
            self.over_z(odd).start()
            self.along_x(0, even)
            self.along_x(0, odd)
            self.over_y(odd).start()
            self.over_z(even).start()

        run(0, 1)
        self.more(0, lambda: run(2, 3))

    def second(self):
        def from_y(even, odd):
            self.over_y(even).wait_recv()
            self.corner(even).start()
            self.along_x(1, even)

        def from_z(even, odd):
            self.over_z(odd).wait_recv()
            self.corner(odd).start()
            self.along_x(2, odd)

        def own(even, odd):
            self.relay_x(0, even)
            self.relay_x(0, odd)

        def late_y(even, odd):
            self.over_y(odd).wait_recv()
            self.along_x(1, odd)

        def late_z(even, odd):
            self.over_z(even).wait_recv()
            self.along_x(2, even)

        for step in (from_y, from_z, own, late_y, late_z):
            step(0, 1)

        def more_here():
            own(2, 3)
            from_y(2, 3)
            late_y(2, 3)

        def more_there():
            from_z(2, 3)
            late_z(2, 3)

        self.more(0, more_here)
        self.more(2, more_there)

    def third(self):
        def corners(even, odd):
            self.corner(even).wait_recv()
            self.along_x(3, even)
            self.corner(odd).wait_recv()
            self.along_x(3, odd)

        def relay(kind, even, odd):
            self.relay_x(kind, even)
            self.relay_x(kind, odd)

        corners(0, 1)
        relay(1, 0, 1)
        relay(2, 0, 1)
        self.more(0, lambda: relay(1, 2, 3))

        def more_there():
            corners(2, 3)
            relay(2, 2, 3)

        self.more(2, more_there)

    def fourth(self):
        def relay(even, odd):
            self.relay_x(3, even)
            self.relay_x(3, odd)

        relay(0, 1)
        self.more(3, lambda: relay(2, 3))

    def last(self, kind):
        def run(even, odd):
            self.to_right(kind, odd).wait_recv()
            self.to_left(kind, even).wait_recv()
            self.onward(kind, even).wait_recv()
            self.onward(kind, odd).wait_recv()

        run(0, 1)
        self.more(kind, lambda: run(2, 3))

    def sent(self):
        def along(kind, even, odd):
            for c in (even, odd):
                self.to_right(kind, c).wait_send()
                self.to_left(kind, c).wait_send()
                self.onward(kind, c).wait_send()

        def across(even, odd):
            for c in (even, odd):
                self.over_y(c).wait_send()
                self.over_z(c).wait_send()

        across(0, 1)
        self.corner(0).wait_send()
        self.corner(1).wait_send()
        for kind in range(4):
            along(kind, 0, 1)

        def more_here():
            across(2, 3)
            self.corner(2).wait_send()
            along(0, 2, 3)
            along(1, 2, 3)

        def more_there():
            self.corner(3).wait_send()
            along(2, 2, 3)
            along(3, 2, 3)

        self.more(0, more_here)
        self.more(2, more_there)


def place_rows(tiles, matrix, box, half):
    rows = pl.ds(pl.multiple_of(half * 4 * ROWS, 4 * ROWS), 4 * ROWS)
    matrix[rows, :] = jnp.zeros((4 * ROWS, POINTS), jnp.float32)
    for x in range(4):
        block = box * 8 + half * 4 + x
        tile = 2 * half + x // 2
        at = pl.ds(pl.multiple_of((half * 4 + x) * ROWS, ROWS), ROWS)
        for t in range(3):
            lanes = pl.ds(pl.multiple_of((tile + t) % 4 * BLOCK, BLOCK), BLOCK)
            matrix[at, lanes] = tiles[block, t] * (0.5 if t == 0 else 1.0)
    return rows


def kernel(t_ref, map_ref, raw_ref, tiles, outer, other_map, near_part, far_part, shuffle, a, panel, send_sem, recv_sem, map_sem):
    sib, leaf = lax.axis_index("sib"), lax.axis_index("leaf")
    leaves = lax.axis_size("leaf")
    x, z = sib % 4, sib // 4
    near = {
        "x": x, "z": z,
        "right": {"sib": z * 4 + (x + 1) % 4},
        "left": {"sib": z * 4 + (x + 3) % 4},
        "across_z": {"sib": (sib + 4) % 8},
        "across_y": {"leaf": (leaf + leaves // 2) % leaves},
    }
    barrier = pltpu.get_barrier_semaphore()
    for name in ("right", "left", "across_z", "across_y"):
        pl.semaphore_signal(barrier, inc=1, device_id=near[name], device_id_type=MESH)
    pl.semaphore_wait(barrier, 4)

    map_copy = pltpu.make_async_remote_copy(
        src_ref=map_ref, dst_ref=other_map, send_sem=map_sem.at[0], recv_sem=map_sem.at[1],
        device_id=near["across_y"], device_id_type=MESH,
    )
    map_copy.start()

    def z_of(kind):
        return z if kind < 2 else 1 - z

    def own_tile(c):
        lanes = pl.ds(pl.multiple_of(POINTS + (sib // 2 + min(c, 2)) % 4 * BLOCK, BLOCK), BLOCK)
        return t_ref.at[:, lanes] if c < 2 else t_ref.at[pl.ds((c - 2) * HALF, HALF), lanes]

    def tile_view(kind, x, c):
        block = tiles.at[kind % 2 * 8 + z_of(kind) * 4 + x, min(c, 2)]
        return block if c < 2 else block.at[pl.ds((c - 2) * HALF, HALF), :]

    def own_rows(c):
        return t_ref.at[pl.ds(c * HALF, HALF), pl.ds(0, POINTS)]

    def row_view(kind, x, c):
        return outer.at[pl.ds(kind % 2 * POINTS + (z_of(kind) * 4 + x) * ROWS + c * HALF, HALF), :]

    g = Exchange(own_tile, tile_view, send_sem.at[0], recv_sem.at[0], near, lambda kind: z_of(kind) == 0)
    r = Exchange(own_rows, row_view, send_sem.at[1], recv_sem.at[1], near, None)
    g.first()
    mine = pl.ds(pl.multiple_of(sib * ROWS, ROWS), ROWS)
    outer[mine, :] = t_ref[:, :POINTS]
    for t in range(2):
        tiles[sib, t] = t_ref[:, pl.ds(pl.multiple_of(POINTS + (sib // 2 + t) % 4 * BLOCK, BLOCK), BLOCK)]

    @pl.when(z == 0)
    def _():
        tiles[sib, 2] = t_ref[:, pl.ds(pl.multiple_of(POINTS + (sib // 2 + 2) % 4 * BLOCK, BLOCK), BLOCK)]

    for block in (4, 5, 6, 7, 12, 13, 14, 15):
        tiles[block, 2] = jnp.zeros((ROWS, BLOCK), jnp.float32)
    g.second()
    map_copy.wait()
    point = lax.broadcasted_iota(jnp.int32, (POINTS, POINTS), 0)
    own_onehot = jnp.where(point == map_ref[...], 1.0, 0.0).astype(jnp.bfloat16)
    other_onehot = jnp.where(point == other_map[...], 1.0, 0.0).astype(jnp.bfloat16)
    shuffle[...] = matmul(own_onehot, other_onehot, ((0,), (0,))).astype(jnp.bfloat16)
    g.third()
    g.fourth()
    r.first()

    def permuted(half):
        rows = place_rows(tiles, far_part, 1, half)
        moved = select_columns(far_part[rows, :], shuffle[...], ((1,), (1,)))
        lanes = pl.ds(pl.multiple_of(half * 4 * ROWS, 4 * ROWS), 4 * ROWS)
        return select_rows(shuffle[:, lanes], moved)

    g.last(1)
    near_part[...] = permuted(z)
    g.last(0)
    place_rows(tiles, a, 0, z)
    g.last(2)
    place_rows(tiles, a, 0, 1 - z)
    g.last(3)
    near_part[...] = (near_part[...] + a[...]) + permuted(1 - z)
    for i in range(4):
        for j in range(4):
            rows, lanes = pl.ds(i * BLOCK, BLOCK), pl.ds(j * BLOCK, BLOCK)
            a[rows, lanes] = near_part[rows, lanes] + near_part[lanes, rows].T

    def finish():
        for kind in range(4):
            r.last(kind)

    for k, step in enumerate((r.second, r.third, r.fourth, finish)):
        eliminate(a, panel, k)
        step()

    wide = outer[pl.ds(0, POINTS), pl.ds(pl.multiple_of(sib // 2 * BLOCK, BLOCK), BLOCK)]
    wide = pltpu.roll(wide, (sib % 2) * ROWS, 1)[:, :ROWS]
    right = product(wide.T, a[...])
    rows = lax.broadcasted_iota(jnp.int32, (ROWS, POINTS), 0) + sib * ROWS
    chosen = select_rows(jnp.where(rows == map_ref[...], 1.0, 0.0).astype(jnp.bfloat16), a[...])
    raw_ref[: 2 * ROWS] = product(jnp.concatenate([right, chosen], axis=0), outer[pl.ds(0, POINTS), :])
    moved = select_columns(right, shuffle[...], ((1,), (0,)))
    raw_ref[2 * ROWS :] = product(moved, outer[pl.ds(POINTS, POINTS), :])
    g.sent()
    r.sent()


def outputs(raw_ref, ext_ref, own_ref, cross_ref, sol_ref):
    own_ref[...] = ext_ref[...] - raw_ref[:ROWS]
    sol_ref[...] = -raw_ref[ROWS : 2 * ROWS]
    cross_ref[...] = -raw_ref[2 * ROWS :]


def on_device(t_int, t_ext, iface_map):
    vmem = pl.BlockSpec(memory_space=pltpu.VMEM)
    raw = pl.pallas_call(
        kernel,
        out_shape=jax.ShapeDtypeStruct((3 * ROWS, POINTS), jnp.float32),
        in_specs=[vmem] * 2,
        out_specs=vmem,
        scratch_shapes=[
            pltpu.VMEM((16, 3, ROWS, BLOCK), jnp.float32),
            pltpu.VMEM((2 * POINTS, POINTS), jnp.float32),
            pltpu.VMEM((1, POINTS), jnp.int32),
            pltpu.VMEM((POINTS, POINTS), jnp.float32),
            pltpu.VMEM((POINTS, POINTS), jnp.float32),
            pltpu.VMEM((POINTS, POINTS), jnp.bfloat16),
            pltpu.VMEM((POINTS, POINTS), jnp.float32),
            pltpu.VMEM((BLOCK, POINTS), jnp.float32),
            pltpu.SemaphoreType.DMA((2, COPIES)),
            pltpu.SemaphoreType.DMA((2, COPIES)),
            pltpu.SemaphoreType.DMA((2,)),
        ],
        compiler_params=pltpu.CompilerParams(collective_id=0, has_side_effects=True),
    )(t_int[0], iface_map)
    block = jax.ShapeDtypeStruct((ROWS, POINTS), jnp.float32)
    outs = pl.pallas_call(outputs, out_shape=(block,) * 3, in_specs=[vmem] * 2, out_specs=(vmem,) * 3)(raw, t_ext[0])
    return tuple(out[None] for out in outs)


def solution(mesh):
    placed = (P("leaf", "sib", None), P("leaf", "sib", None), P("leaf", None))
    return jax.shard_map(
        on_device,
        mesh=mesh,
        in_specs=placed,
        out_specs=(P("leaf", "sib", None),) * 3,
        check_vma=False,
    )
```

```python
import jax
import jax.numpy as jnp
from jax import lax
from jax.experimental import pallas as pl
from jax.experimental.pallas import tpu as pltpu
from jax.sharding import PartitionSpec as P

MESH = pl.DeviceIdType.MESH
POINTS = 512
ROWS = 64
HALF = 32
BLOCK = 128
PANEL = 2
STRIPS = BLOCK // 8
XR, XL, XO, Y, Z, YC, ZC = 0, 16, 32, 48, 52, 56, 60
COPIES = 64


def matmul(a, b, dims=((1,), (0,))):
    return lax.dot_general(a, b, (dims, ((), ())), preferred_element_type=jnp.float32)


def exact_matmul(a, b):
    return jnp.dot(a, b, precision=lax.Precision.HIGHEST, preferred_element_type=jnp.float32)


def thirds(x):
    high = x.astype(jnp.bfloat16)
    rest = x - high.astype(jnp.float32)
    mid = rest.astype(jnp.bfloat16)
    low = (rest - mid.astype(jnp.float32)).astype(jnp.bfloat16)
    return high, mid, low


def halves(x):
    high = x.astype(jnp.bfloat16)
    return high, (x - high.astype(jnp.float32)).astype(jnp.bfloat16)


def select_rows(onehot, x):
    high, mid, low = thirds(x)
    return matmul(onehot, high) + (matmul(onehot, mid) + matmul(onehot, low))


def select_columns(x, onehot, dims):
    high, mid, low = thirds(x)
    return matmul(high, onehot, dims) + (matmul(mid, onehot, dims) + matmul(low, onehot, dims))


def product(a, b):
    a_high, a_low = halves(a)
    b_high, b_low = halves(b)
    return matmul(a_high, b_high) + (matmul(a_high, b_low) + matmul(a_low, b_high))


def pivot_panel(own, first):
    lane = lax.broadcasted_iota(jnp.int32, (8, BLOCK), 1)
    sub = lax.broadcasted_iota(jnp.int32, (8, BLOCK), 0)
    width = 8 * len(own)
    cols = [[column_of(x, 8 * first + j) for x in own] for j in range(width)]
    pivots = (lane >= 8 * first) & (lane < 8 * first + width)
    s = [jnp.where(pivots, jnp.where(lane - 8 * (first + n) == sub, 1.0, 0.0), x) for n, x in enumerate(own)]
    for j in range(width):
        at, row = divmod(j, 8)
        here = sub == row
        inverse = 1.0 / row_of(cols[j][at], row)
        factor = [jnp.where(here, -1.0, x) if n == at else x for n, x in enumerate(cols[j])]

        def reduced(xs):
            r = row_of(xs[at], row)
            return [(jnp.where(here, 0.0, x) if n == at else x) - (f * r) * inverse for n, (x, f) in enumerate(zip(xs, factor))]

        for q in range(j + 1, width):
            cols[q] = reduced(cols[q])
        s = reduced(s)
    return s, pivots


def row_of(x, j):
    return jnp.broadcast_to(x[j : j + 1, :], (8, BLOCK))


def column_of(x, lane):
    return jnp.broadcast_to(x[:, lane : lane + 1], (8, BLOCK))


def block_inverse(strips):
    strips = list(strips)
    for k in range(0, STRIPS, PANEL):
        s, pivots = pivot_panel(strips[k : k + PANEL], k)
        soon = range(k + PANEL, min(STRIPS, k + 2 * PANEL))
        rest = [i for i in range(STRIPS) if not k <= i < k + PANEL and i not in soon]
        old = list(strips)
        for i in soon:
            t = [column_of(old[i], 8 * k + j) * row_of(s[j // 8], j % 8) for j in range(8 * PANEL)]
            while len(t) > 1:
                t = [t[n] + t[n + 1] for n in range(0, len(t), 2)]
            strips[i] = jnp.where(pivots, 0.0, old[i]) - t[0]
        left = jnp.concatenate([jnp.where(pivots, old[i], 0.0) for i in rest], axis=0)
        zero = jnp.zeros((8, BLOCK), jnp.float32)
        right = jnp.concatenate([s[i - k] if k <= i < k + PANEL else zero for i in range(STRIPS)], axis=0)
        change = exact_matmul(left, right)
        for n, i in enumerate(rest):
            strips[i] = jnp.where(pivots, 0.0, old[i]) - change[8 * n : 8 * n + 8]
        strips[k : k + PANEL] = s
    return jnp.concatenate(strips, axis=0)


def invert(a, panel, between):
    diagonal = [a[pl.ds(8 * i, 8), pl.ds(0, BLOCK)] for i in range(STRIPS)]
    for k in range(POINTS // BLOCK):
        at, after = pl.ds(k * BLOCK, BLOCK), pl.ds((k + 1) * BLOCK, BLOCK)
        inverse = block_inverse(diagonal)
        between[2 * k]()
        if (k + 1) * BLOCK < POINTS:
            ahead = a[after, after] - exact_matmul(a[after, at], exact_matmul(inverse, a[at, after]))
            diagonal = [ahead[8 * i : 8 * i + 8] for i in range(STRIPS)]
        panel[...] = exact_matmul(inverse, a[at, :])
        panel[:, at] = inverse
        a[at, at] = jnp.zeros((BLOCK, BLOCK), jnp.float32)
        column = a[:, at]
        a[:, at] = jnp.zeros((POINTS, BLOCK), jnp.float32)
        a[...] = a[...] - exact_matmul(column, panel[...])
        a[at, :] = panel[...]
        between[2 * k + 1]()


class Exchange:
    def __init__(self, own, view, send_sem, recv_sem, near, has_more):
        self.own, self.view, self.near, self.has_more = own, view, near, has_more
        self.send_sem, self.recv_sem = send_sem, recv_sem

    def copy(self, index, src, dst, to):
        return pltpu.make_async_remote_copy(
            src_ref=src, dst_ref=dst, send_sem=self.send_sem.at[index], recv_sem=self.recv_sem.at[index],
            device_id=self.near[to], device_id_type=MESH,
        )

    def over_y(self, c):
        return self.copy(Y + c, self.own(c), self.view(1, self.near["x"], c), "across_y")

    def over_z(self, c):
        return self.copy(Z + c, self.own(c), self.view(0, self.near["x"], c), "across_z")

    def corner(self, c):
        x = self.near["x"]
        if c % 2:
            return self.copy(YC + c, self.view(2, x, c), self.view(3, x, c), "across_y")
        return self.copy(ZC + c, self.view(1, x, c), self.view(1, x, c), "across_z")

    def to_right(self, kind, c):
        x = self.near["x"]
        src = self.own(c) if kind == 0 else self.view(kind, x, c)
        return self.copy(XR + 4 * kind + c, src, self.view(kind, x, c), "right")

    def to_left(self, kind, c):
        x = self.near["x"]
        src = self.own(c) if kind == 0 else self.view(kind, x, c)
        return self.copy(XL + 4 * kind + c, src, self.view(kind, x, c), "left")

    def to_opposite(self, kind, c):
        x = self.near["x"]
        src = self.own(c) if kind == 0 else self.view(kind, x, c)
        return self.copy(XO + 4 * kind + c, src, self.view(kind, x, c), "opposite")

    def along_x(self, kind, c):
        self.to_right(kind, c).start()
        self.to_left(kind, c).start()
        self.to_opposite(kind, c).start()

    def more(self, kind, run):
        if self.has_more is not None:
            pl.when(self.has_more(kind))(run)

    def first(self):
        def run(even, odd):
            self.over_y(even).start()
            self.over_z(odd).start()
            self.along_x(0, even)
            self.along_x(0, odd)
            self.over_y(odd).start()
            self.over_z(even).start()

        run(0, 1)
        self.more(0, lambda: run(2, 3))

    def second(self):
        def from_y(even, odd):
            self.over_y(even).wait_recv()
            self.corner(even).start()
            self.along_x(1, even)

        def from_z(even, odd):
            self.over_z(odd).wait_recv()
            self.corner(odd).start()
            self.along_x(2, odd)

        def late_y(even, odd):
            self.over_y(odd).wait_recv()
            self.along_x(1, odd)

        def late_z(even, odd):
            self.over_z(even).wait_recv()
            self.along_x(2, even)

        for step in (from_y, from_z, late_y, late_z):
            step(0, 1)

        def more_here():
            from_y(2, 3)
            late_y(2, 3)

        def more_there():
            from_z(2, 3)
            late_z(2, 3)

        self.more(0, more_here)
        self.more(2, more_there)

    def third(self):
        def corners(even, odd):
            self.corner(even).wait_recv()
            self.along_x(3, even)
            self.corner(odd).wait_recv()
            self.along_x(3, odd)

        corners(0, 1)
        self.more(2, lambda: corners(2, 3))

    def last(self, kind):
        def run(even, odd):
            for c in (even, odd):
                self.to_right(kind, c).wait_recv()
                self.to_left(kind, c).wait_recv()
                self.to_opposite(kind, c).wait_recv()

        run(0, 1)
        self.more(kind, lambda: run(2, 3))

    def sent(self):
        def along(kind, even, odd):
            for c in (even, odd):
                self.to_right(kind, c).wait_send()
                self.to_left(kind, c).wait_send()
                self.to_opposite(kind, c).wait_send()

        def across(even, odd):
            for c in (even, odd):
                self.over_y(c).wait_send()
                self.over_z(c).wait_send()

        across(0, 1)
        self.corner(0).wait_send()
        self.corner(1).wait_send()
        for kind in range(4):
            along(kind, 0, 1)

        def more_here():
            across(2, 3)
            self.corner(2).wait_send()
            along(0, 2, 3)
            along(1, 2, 3)

        def more_there():
            self.corner(3).wait_send()
            along(2, 2, 3)
            along(3, 2, 3)

        self.more(0, more_here)
        self.more(2, more_there)


def place_rows(tiles, matrix, box, half):
    rows = pl.ds(pl.multiple_of(half * 4 * ROWS, 4 * ROWS), 4 * ROWS)
    matrix[rows, :] = jnp.zeros((4 * ROWS, POINTS), jnp.float32)
    for x in range(4):
        block = box * 8 + half * 4 + x
        tile = 2 * half + x // 2
        at = pl.ds(pl.multiple_of((half * 4 + x) * ROWS, ROWS), ROWS)
        for t in range(3):
            lanes = pl.ds(pl.multiple_of((tile + t) % 4 * BLOCK, BLOCK), BLOCK)
            matrix[at, lanes] = tiles[block, t] * (0.5 if t == 0 else 1.0)
    return rows


def kernel(t_ref, map_ref, raw_ref, tiles, outer, other_map, near_part, far_part, shuffle, a, panel, send_sem, recv_sem, map_sem, keep_sem):
    sib, leaf = lax.axis_index("sib"), lax.axis_index("leaf")
    leaves = lax.axis_size("leaf")
    x, z = sib % 4, sib // 4
    near = {
        "x": x, "z": z,
        "right": {"sib": z * 4 + (x + 1) % 4},
        "left": {"sib": z * 4 + (x + 3) % 4},
        "opposite": {"sib": z * 4 + (x + 2) % 4},
        "across_z": {"sib": (sib + 4) % 8},
        "across_y": {"leaf": (leaf + leaves // 2) % leaves},
    }
    barrier = pltpu.get_barrier_semaphore()
    for name in ("right", "left", "opposite", "across_z", "across_y"):
        pl.semaphore_signal(barrier, inc=1, device_id=near[name], device_id_type=MESH)
    pl.semaphore_wait(barrier, 5)

    map_copy = pltpu.make_async_remote_copy(
        src_ref=map_ref, dst_ref=other_map, send_sem=map_sem.at[0], recv_sem=map_sem.at[1],
        device_id=near["across_y"], device_id_type=MESH,
    )
    map_copy.start()

    def z_of(kind):
        return z if kind < 2 else 1 - z

    def own_tile(c):
        lanes = pl.ds(pl.multiple_of(POINTS + (sib // 2 + min(c, 2)) % 4 * BLOCK, BLOCK), BLOCK)
        return t_ref.at[:, lanes] if c < 2 else t_ref.at[pl.ds((c - 2) * HALF, HALF), lanes]

    def tile_view(kind, x, c):
        block = tiles.at[kind % 2 * 8 + z_of(kind) * 4 + x, min(c, 2)]
        return block if c < 2 else block.at[pl.ds((c - 2) * HALF, HALF), :]

    def own_rows(c):
        return t_ref.at[pl.ds(c * HALF, HALF), pl.ds(0, POINTS)]

    def row_view(kind, x, c):
        return outer.at[pl.ds(kind % 2 * POINTS + (z_of(kind) * 4 + x) * ROWS + c * HALF, HALF), :]

    g = Exchange(own_tile, tile_view, send_sem.at[0], recv_sem.at[0], near, lambda kind: z_of(kind) == 0)
    r = Exchange(own_rows, row_view, send_sem.at[1], recv_sem.at[1], near, None)
    g.first()

    def keep(n):
        if n == 3:
            mine = pl.ds(pl.multiple_of(sib * ROWS, ROWS), ROWS)
            return pltpu.make_async_copy(t_ref.at[:, pl.ds(0, POINTS)], outer.at[mine, :], keep_sem.at[n])
        lanes = pl.ds(pl.multiple_of(POINTS + (sib // 2 + n) % 4 * BLOCK, BLOCK), BLOCK)
        return pltpu.make_async_copy(t_ref.at[:, lanes], tiles.at[sib, n], keep_sem.at[n])

    for n in (0, 1, 3):
        keep(n).start()
    pl.when(z == 0)(lambda: keep(2).start())

    for block in (4, 5, 6, 7, 12, 13, 14, 15):
        tiles[block, 2] = jnp.zeros((ROWS, BLOCK), jnp.float32)
    g.second()
    map_copy.wait()
    point = lax.broadcasted_iota(jnp.int32, (POINTS, POINTS), 0)
    own_onehot = jnp.where(point == map_ref[...], 1.0, 0.0).astype(jnp.bfloat16)
    other_onehot = jnp.where(point == other_map[...], 1.0, 0.0).astype(jnp.bfloat16)
    shuffle[...] = matmul(own_onehot, other_onehot, ((0,), (0,))).astype(jnp.bfloat16)
    g.third()
    r.first()
    for n in (0, 1, 3):
        keep(n).wait()
    pl.when(z == 0)(lambda: keep(2).wait())

    def permuted(half):
        rows = place_rows(tiles, far_part, 1, half)
        moved = select_columns(far_part[rows, :], shuffle[...], ((1,), (1,)))
        lanes = pl.ds(pl.multiple_of(half * 4 * ROWS, 4 * ROWS), 4 * ROWS)
        return select_rows(shuffle[:, lanes], moved)

    g.last(1)
    near_part[...] = permuted(z)
    g.last(0)
    place_rows(tiles, a, 0, z)
    g.last(2)
    place_rows(tiles, a, 0, 1 - z)
    g.last(3)
    near_part[...] = (near_part[...] + a[...]) + permuted(1 - z)
    for i in range(4):
        for j in range(4):
            rows, lanes = pl.ds(i * BLOCK, BLOCK), pl.ds(j * BLOCK, BLOCK)
            a[rows, lanes] = near_part[rows, lanes] + near_part[lanes, rows].T

    def nothing():
        pass

    invert(a, panel, (r.second, nothing, nothing, r.third, nothing, nothing, nothing, nothing))

    rows = lax.broadcasted_iota(jnp.int32, (ROWS, POINTS), 0) + sib * ROWS
    chosen = select_rows(jnp.where(rows == map_ref[...], 1.0, 0.0).astype(jnp.bfloat16), a[...])
    r.last(0)
    r.last(2)
    wide = outer[pl.ds(0, POINTS), pl.ds(pl.multiple_of(sib // 2 * BLOCK, BLOCK), BLOCK)]
    wide = pltpu.roll(wide, (sib % 2) * ROWS, 1)[:, :ROWS]
    right = product(wide.T, a[...])
    raw_ref[: 2 * ROWS] = product(jnp.concatenate([right, chosen], axis=0), outer[pl.ds(0, POINTS), :])
    moved = select_columns(right, shuffle[...], ((1,), (0,)))
    r.last(1)
    r.last(3)
    raw_ref[2 * ROWS :] = product(moved, outer[pl.ds(POINTS, POINTS), :])
    g.sent()
    r.sent()


def outputs(raw_ref, ext_ref, own_ref, cross_ref, sol_ref):
    own_ref[...] = ext_ref[...] - raw_ref[:ROWS]
    sol_ref[...] = -raw_ref[ROWS : 2 * ROWS]
    cross_ref[...] = -raw_ref[2 * ROWS :]


def on_device(t_int, t_ext, iface_map):
    vmem = pl.BlockSpec(memory_space=pltpu.VMEM)
    raw = pl.pallas_call(
        kernel,
        out_shape=jax.ShapeDtypeStruct((3 * ROWS, POINTS), jnp.float32),
        in_specs=[pl.BlockSpec(memory_space=pl.ANY), vmem],
        out_specs=vmem,
        scratch_shapes=[
            pltpu.VMEM((16, 3, ROWS, BLOCK), jnp.float32),
            pltpu.VMEM((2 * POINTS, POINTS), jnp.float32),
            pltpu.VMEM((1, POINTS), jnp.int32),
            pltpu.VMEM((POINTS, POINTS), jnp.float32),
            pltpu.VMEM((POINTS, POINTS), jnp.float32),
            pltpu.VMEM((POINTS, POINTS), jnp.bfloat16),
            pltpu.VMEM((POINTS, POINTS), jnp.float32),
            pltpu.VMEM((BLOCK, POINTS), jnp.float32),
            pltpu.SemaphoreType.DMA((2, COPIES)),
            pltpu.SemaphoreType.DMA((2, COPIES)),
            pltpu.SemaphoreType.DMA((2,)),
            pltpu.SemaphoreType.DMA((4,)),
        ],
        compiler_params=pltpu.CompilerParams(collective_id=0, has_side_effects=True),
    )(t_int[0], iface_map)
    block = jax.ShapeDtypeStruct((ROWS, POINTS), jnp.float32)
    outs = pl.pallas_call(outputs, out_shape=(block,) * 3, in_specs=[vmem] * 2, out_specs=(vmem,) * 3)(raw, t_ext[0])
    return tuple(out[None] for out in outs)


def solution(mesh):
    placed = (P("leaf", "sib", None), P("leaf", "sib", None), P("leaf", None))
    return jax.shard_map(
        on_device,
        mesh=mesh,
        in_specs=placed,
        out_specs=(P("leaf", "sib", None),) * 3,
        check_vma=False,
    )
```

```python
import jax
import jax.numpy as jnp
from jax import lax
from jax.experimental import pallas as pl
from jax.experimental.pallas import tpu as pltpu
from jax.sharding import PartitionSpec as P

MESH = pl.DeviceIdType.MESH
POINTS = 512
ROWS = 64
HALF = 32
BLOCK = 128
PANEL = 2
STRIPS = BLOCK // 8
XR, XL, XO, Y, Z, YC, ZC = 0, 16, 32, 48, 52, 56, 60
COPIES = 64


def matmul(a, b, dims=((1,), (0,))):
    return lax.dot_general(a, b, (dims, ((), ())), preferred_element_type=jnp.float32)


def exact_matmul(a, b):
    return jnp.dot(a, b, precision=lax.Precision.HIGHEST, preferred_element_type=jnp.float32)


def thirds(x):
    high = x.astype(jnp.bfloat16)
    rest = x - high.astype(jnp.float32)
    mid = rest.astype(jnp.bfloat16)
    low = (rest - mid.astype(jnp.float32)).astype(jnp.bfloat16)
    return high, mid, low


def halves(x):
    high = x.astype(jnp.bfloat16)
    return high, (x - high.astype(jnp.float32)).astype(jnp.bfloat16)


def select_rows(onehot, x):
    high, mid, low = thirds(x)
    return matmul(onehot, high) + (matmul(onehot, mid) + matmul(onehot, low))


def select_columns(x, onehot, dims):
    high, mid, low = thirds(x)
    return matmul(high, onehot, dims) + (matmul(mid, onehot, dims) + matmul(low, onehot, dims))


def product(a, b):
    a_high, a_low = halves(a)
    b_high, b_low = halves(b)
    return matmul(a_high, b_high) + (matmul(a_high, b_low) + matmul(a_low, b_high))


def pivot_panel(own, first):
    lane = lax.broadcasted_iota(jnp.int32, (8, BLOCK), 1)
    sub = lax.broadcasted_iota(jnp.int32, (8, BLOCK), 0)
    width = 8 * len(own)
    cols = [[column_of(x, 8 * first + j) for x in own] for j in range(width)]
    pivots = (lane >= 8 * first) & (lane < 8 * first + width)
    s = [jnp.where(pivots, jnp.where(lane - 8 * (first + n) == sub, 1.0, 0.0), x) for n, x in enumerate(own)]
    for j in range(width):
        at, row = divmod(j, 8)
        here = sub == row
        inverse = 1.0 / row_of(cols[j][at], row)
        factor = [jnp.where(here, -1.0, x) if n == at else x for n, x in enumerate(cols[j])]

        def reduced(xs):
            r = row_of(xs[at], row)
            return [(jnp.where(here, 0.0, x) if n == at else x) - (f * r) * inverse for n, (x, f) in enumerate(zip(xs, factor))]

        for q in range(j + 1, width):
            cols[q] = reduced(cols[q])
        s = reduced(s)
    return s, pivots


def row_of(x, j):
    return jnp.broadcast_to(x[j : j + 1, :], (8, BLOCK))


def column_of(x, lane):
    return jnp.broadcast_to(x[:, lane : lane + 1], (8, BLOCK))


def block_inverse(strips):
    strips = list(strips)
    for k in range(0, STRIPS, PANEL):
        s, pivots = pivot_panel(strips[k : k + PANEL], k)
        soon = range(k + PANEL, min(STRIPS, k + 2 * PANEL))
        rest = [i for i in range(STRIPS) if not k <= i < k + PANEL and i not in soon]
        old = list(strips)
        for i in soon:
            t = [column_of(old[i], 8 * k + j) * row_of(s[j // 8], j % 8) for j in range(8 * PANEL)]
            while len(t) > 1:
                t = [t[n] + t[n + 1] for n in range(0, len(t), 2)]
            strips[i] = jnp.where(pivots, 0.0, old[i]) - t[0]
        left = jnp.concatenate([jnp.where(pivots, old[i], 0.0) for i in rest], axis=0)
        zero = jnp.zeros((8, BLOCK), jnp.float32)
        right = jnp.concatenate([s[i - k] if k <= i < k + PANEL else zero for i in range(STRIPS)], axis=0)
        change = exact_matmul(left, right)
        for n, i in enumerate(rest):
            strips[i] = jnp.where(pivots, 0.0, old[i]) - change[8 * n : 8 * n + 8]
        strips[k : k + PANEL] = s
    return jnp.concatenate(strips, axis=0)


def invert(a, panel, between):
    diagonal = [a[pl.ds(8 * i, 8), pl.ds(0, BLOCK)] for i in range(STRIPS)]
    for k in range(POINTS // BLOCK):
        at, after = pl.ds(k * BLOCK, BLOCK), pl.ds((k + 1) * BLOCK, BLOCK)
        inverse = block_inverse(diagonal)
        between[2 * k]()
        if (k + 1) * BLOCK < POINTS:
            ahead = a[after, after] - exact_matmul(a[after, at], exact_matmul(inverse, a[at, after]))
            diagonal = [ahead[8 * i : 8 * i + 8] for i in range(STRIPS)]
        panel[...] = exact_matmul(inverse, a[at, :])
        panel[:, at] = inverse
        a[at, at] = jnp.zeros((BLOCK, BLOCK), jnp.float32)
        column = a[:, at]
        a[:, at] = jnp.zeros((POINTS, BLOCK), jnp.float32)
        a[...] = a[...] - exact_matmul(column, panel[...])
        a[at, :] = panel[...]
        between[2 * k + 1]()


class Exchange:
    def __init__(self, own, view, send_sem, recv_sem, near, has_more, relayed):
        self.own, self.view, self.near, self.has_more, self.relayed = own, view, near, has_more, relayed
        self.send_sem, self.recv_sem = send_sem, recv_sem

    def copy(self, index, src, dst, to):
        return pltpu.make_async_remote_copy(
            src_ref=src, dst_ref=dst, send_sem=self.send_sem.at[index], recv_sem=self.recv_sem.at[index],
            device_id=self.near[to], device_id_type=MESH,
        )

    def over_y(self, c):
        return self.copy(Y + c, self.own(c), self.view(1, self.near["x"], c), "across_y")

    def over_z(self, c):
        return self.copy(Z + c, self.own(c), self.view(0, self.near["x"], c), "across_z")

    def corner(self, c):
        x = self.near["x"]
        if c % 2:
            return self.copy(YC + c, self.view(2, x, c), self.view(3, x, c), "across_y")
        return self.copy(ZC + c, self.view(1, x, c), self.view(1, x, c), "across_z")

    def to_right(self, kind, c):
        x = self.near["x"]
        src = self.own(c) if kind == 0 else self.view(kind, x, c)
        return self.copy(XR + 4 * kind + c, src, self.view(kind, x, c), "right")

    def to_left(self, kind, c):
        x = self.near["x"]
        src = self.own(c) if kind == 0 else self.view(kind, x, c)
        return self.copy(XL + 4 * kind + c, src, self.view(kind, x, c), "left")

    def to_opposite(self, kind, c):
        x = self.near["x"]
        if self.relayed:
            block = self.view(kind, (x + (1 if c % 2 else 3)) % 4, c)
            return self.copy(XO + 4 * kind + c, block, block, "left" if c % 2 else "right")
        src = self.own(c) if kind == 0 else self.view(kind, x, c)
        return self.copy(XO + 4 * kind + c, src, self.view(kind, x, c), "opposite")

    def along_x(self, kind, c):
        self.to_right(kind, c).start()
        self.to_left(kind, c).start()
        if not self.relayed:
            self.to_opposite(kind, c).start()

    def relay(self, kind):
        self.to_right(kind, 0).wait_recv()
        self.to_opposite(kind, 0).start()
        self.to_left(kind, 1).wait_recv()
        self.to_opposite(kind, 1).start()

    def more(self, kind, run):
        if self.has_more is not None:
            pl.when(self.has_more(kind))(run)

    def first(self):
        def run(even, odd):
            self.over_y(even).start()
            self.over_z(odd).start()
            self.along_x(0, even)
            self.along_x(0, odd)
            self.over_y(odd).start()
            self.over_z(even).start()

        run(0, 1)
        self.more(0, lambda: run(2, 3))

    def second(self):
        def from_y(even, odd):
            self.over_y(even).wait_recv()
            self.corner(even).start()
            self.along_x(1, even)

        def from_z(even, odd):
            self.over_z(odd).wait_recv()
            self.corner(odd).start()
            self.along_x(2, odd)

        def late_y(even, odd):
            self.over_y(odd).wait_recv()
            self.along_x(1, odd)

        def late_z(even, odd):
            self.over_z(even).wait_recv()
            self.along_x(2, even)

        for step in (from_y, from_z, late_y, late_z):
            step(0, 1)

        def more_here():
            from_y(2, 3)
            late_y(2, 3)

        def more_there():
            from_z(2, 3)
            late_z(2, 3)

        self.more(0, more_here)
        self.more(2, more_there)

    def third(self):
        def corners(even, odd):
            self.corner(even).wait_recv()
            self.along_x(3, even)
            self.corner(odd).wait_recv()
            self.along_x(3, odd)

        corners(0, 1)
        self.more(2, lambda: corners(2, 3))

    def last(self, kind):
        def run(even, odd):
            for c in (even, odd):
                if c % 2 or not self.relayed:
                    self.to_right(kind, c).wait_recv()
                if c % 2 == 0 or not self.relayed:
                    self.to_left(kind, c).wait_recv()
                self.to_opposite(kind, c).wait_recv()

        run(0, 1)
        self.more(kind, lambda: run(2, 3))

    def sent(self):
        def along(kind, even, odd):
            for c in (even, odd):
                self.to_right(kind, c).wait_send()
                self.to_left(kind, c).wait_send()
                self.to_opposite(kind, c).wait_send()

        def across(even, odd):
            for c in (even, odd):
                self.over_y(c).wait_send()
                self.over_z(c).wait_send()

        across(0, 1)
        self.corner(0).wait_send()
        self.corner(1).wait_send()
        for kind in range(4):
            along(kind, 0, 1)

        def more_here():
            across(2, 3)
            self.corner(2).wait_send()
            along(0, 2, 3)
            along(1, 2, 3)

        def more_there():
            self.corner(3).wait_send()
            along(2, 2, 3)
            along(3, 2, 3)

        self.more(0, more_here)
        self.more(2, more_there)


def place_rows(tiles, matrix, box, half):
    rows = pl.ds(pl.multiple_of(half * 4 * ROWS, 4 * ROWS), 4 * ROWS)
    matrix[rows, :] = jnp.zeros((4 * ROWS, POINTS), jnp.float32)
    for x in range(4):
        block = box * 8 + half * 4 + x
        tile = 2 * half + x // 2
        at = pl.ds(pl.multiple_of((half * 4 + x) * ROWS, ROWS), ROWS)
        for t in range(3):
            lanes = pl.ds(pl.multiple_of((tile + t) % 4 * BLOCK, BLOCK), BLOCK)
            matrix[at, lanes] = tiles[block, t] * (0.5 if t == 0 else 1.0)
    return rows


def kernel(t_ref, map_ref, ext_ref, raw_ref, tiles, outer, other_map, near_part, far_part, shuffle, a, panel, send_sem, recv_sem, map_sem, keep_sem):
    sib, leaf = lax.axis_index("sib"), lax.axis_index("leaf")
    leaves = lax.axis_size("leaf")
    x, z = sib % 4, sib // 4
    near = {
        "x": x, "z": z,
        "right": {"sib": z * 4 + (x + 1) % 4},
        "left": {"sib": z * 4 + (x + 3) % 4},
        "opposite": {"sib": z * 4 + (x + 2) % 4},
        "across_z": {"sib": (sib + 4) % 8},
        "across_y": {"leaf": (leaf + leaves // 2) % leaves},
    }
    barrier = pltpu.get_barrier_semaphore()
    for name in ("right", "left", "opposite", "across_z", "across_y"):
        pl.semaphore_signal(barrier, inc=1, device_id=near[name], device_id_type=MESH)
    pl.semaphore_wait(barrier, 5)

    map_copy = pltpu.make_async_remote_copy(
        src_ref=map_ref, dst_ref=other_map, send_sem=map_sem.at[0], recv_sem=map_sem.at[1],
        device_id=near["across_y"], device_id_type=MESH,
    )
    map_copy.start()

    def z_of(kind):
        return z if kind < 2 else 1 - z

    def own_tile(c):
        lanes = pl.ds(pl.multiple_of(POINTS + (sib // 2 + min(c, 2)) % 4 * BLOCK, BLOCK), BLOCK)
        return t_ref.at[:, lanes] if c < 2 else t_ref.at[pl.ds((c - 2) * HALF, HALF), lanes]

    def tile_view(kind, x, c):
        block = tiles.at[kind % 2 * 8 + z_of(kind) * 4 + x, min(c, 2)]
        return block if c < 2 else block.at[pl.ds((c - 2) * HALF, HALF), :]

    def own_rows(c):
        return t_ref.at[pl.ds(c * HALF, HALF), pl.ds(0, POINTS)]

    def row_view(kind, x, c):
        return outer.at[pl.ds(kind % 2 * POINTS + (z_of(kind) * 4 + x) * ROWS + c * HALF, HALF), :]

    g = Exchange(own_tile, tile_view, send_sem.at[0], recv_sem.at[0], near, lambda kind: z_of(kind) == 0, False)
    r = Exchange(own_rows, row_view, send_sem.at[1], recv_sem.at[1], near, None, True)
    g.first()

    def keep(n):
        if n == 3:
            mine = pl.ds(pl.multiple_of(sib * ROWS, ROWS), ROWS)
            return pltpu.make_async_copy(t_ref.at[:, pl.ds(0, POINTS)], outer.at[mine, :], keep_sem.at[n])
        lanes = pl.ds(pl.multiple_of(POINTS + (sib // 2 + n) % 4 * BLOCK, BLOCK), BLOCK)
        return pltpu.make_async_copy(t_ref.at[:, lanes], tiles.at[sib, n], keep_sem.at[n])

    for n in (0, 1, 3):
        keep(n).start()
    ext_copy = pltpu.make_async_copy(ext_ref, raw_ref.at[pl.ds(0, ROWS), :], keep_sem.at[4])
    ext_copy.start()
    pl.when(z == 0)(lambda: keep(2).start())

    for block in (4, 5, 6, 7, 12, 13, 14, 15):
        tiles[block, 2] = jnp.zeros((ROWS, BLOCK), jnp.float32)
    g.second()
    map_copy.wait()
    point = lax.broadcasted_iota(jnp.int32, (POINTS, POINTS), 0)
    own_onehot = jnp.where(point == map_ref[...], 1.0, 0.0).astype(jnp.bfloat16)
    other_onehot = jnp.where(point == other_map[...], 1.0, 0.0).astype(jnp.bfloat16)
    shuffle[...] = matmul(own_onehot, other_onehot, ((0,), (0,))).astype(jnp.bfloat16)
    g.third()
    r.first()
    for n in (0, 1, 3):
        keep(n).wait()
    ext_copy.wait()
    pl.when(z == 0)(lambda: keep(2).wait())

    def permuted(half):
        rows = place_rows(tiles, far_part, 1, half)
        moved = select_columns(far_part[rows, :], shuffle[...], ((1,), (1,)))
        lanes = pl.ds(pl.multiple_of(half * 4 * ROWS, 4 * ROWS), 4 * ROWS)
        return select_rows(shuffle[:, lanes], moved)

    g.last(1)
    near_part[...] = permuted(z)
    g.last(0)
    place_rows(tiles, a, 0, z)
    g.last(2)
    place_rows(tiles, a, 0, 1 - z)
    g.last(3)
    near_part[...] = (near_part[...] + a[...]) + permuted(1 - z)
    for i in range(4):
        for j in range(4):
            rows, lanes = pl.ds(i * BLOCK, BLOCK), pl.ds(j * BLOCK, BLOCK)
            a[rows, lanes] = near_part[rows, lanes] + near_part[lanes, rows].T

    def nothing():
        pass


    def second():
        r.second()
        r.relay(0)

    def third():
        r.third()
        r.relay(1)
        r.relay(2)

    def fourth():
        r.relay(3)

    invert(a, panel, (second, nothing, nothing, third, nothing, fourth, nothing, nothing))

    rows = lax.broadcasted_iota(jnp.int32, (ROWS, POINTS), 0) + sib * ROWS
    chosen = select_rows(jnp.where(rows == map_ref[...], 1.0, 0.0).astype(jnp.bfloat16), a[...])
    r.last(0)
    r.last(2)
    wide = outer[pl.ds(0, POINTS), pl.ds(pl.multiple_of(sib // 2 * BLOCK, BLOCK), BLOCK)]
    wide = pltpu.roll(wide, (sib % 2) * ROWS, 1)[:, :ROWS]
    right = product(wide.T, a[...])
    both = product(jnp.concatenate([right, chosen], axis=0), outer[pl.ds(0, POINTS), :])
    raw_ref[:ROWS] = raw_ref[:ROWS] - both[:ROWS]
    raw_ref[2 * ROWS :] = -both[ROWS:]
    moved = select_columns(right, shuffle[...], ((1,), (0,)))
    r.last(1)
    r.last(3)
    raw_ref[ROWS : 2 * ROWS] = -product(moved, outer[pl.ds(POINTS, POINTS), :])
    g.sent()
    r.sent()


def outputs(raw_ref, own_ref, cross_ref, sol_ref, sem):
    copies = [
        pltpu.make_async_copy(raw_ref.at[pl.ds(n * ROWS, ROWS), :], out, sem.at[n])
        for n, out in enumerate((own_ref, cross_ref, sol_ref))
    ]
    for copy in copies:
        copy.start()
    for copy in copies:
        copy.wait()


def on_device(t_int, t_ext, iface_map):
    vmem = pl.BlockSpec(memory_space=pltpu.VMEM)
    anywhere = pl.BlockSpec(memory_space=pl.ANY)
    raw = pl.pallas_call(
        kernel,
        out_shape=pltpu.VMEM((3 * ROWS, POINTS), jnp.float32),
        in_specs=[anywhere, vmem, anywhere],
        out_specs=vmem,
        scratch_shapes=[
            pltpu.VMEM((16, 3, ROWS, BLOCK), jnp.float32),
            pltpu.VMEM((2 * POINTS, POINTS), jnp.float32),
            pltpu.VMEM((1, POINTS), jnp.int32),
            pltpu.VMEM((POINTS, POINTS), jnp.float32),
            pltpu.VMEM((POINTS, POINTS), jnp.float32),
            pltpu.VMEM((POINTS, POINTS), jnp.bfloat16),
            pltpu.VMEM((POINTS, POINTS), jnp.float32),
            pltpu.VMEM((BLOCK, POINTS), jnp.float32),
            pltpu.SemaphoreType.DMA((2, COPIES)),
            pltpu.SemaphoreType.DMA((2, COPIES)),
            pltpu.SemaphoreType.DMA((2,)),
            pltpu.SemaphoreType.DMA((5,)),
        ],
        compiler_params=pltpu.CompilerParams(collective_id=0, has_side_effects=True),
    )(t_int[0], iface_map, t_ext[0])
    block = jax.ShapeDtypeStruct((ROWS, POINTS), jnp.float32)
    outs = pl.pallas_call(
        outputs,
        out_shape=(block,) * 3,
        in_specs=[vmem],
        out_specs=(anywhere,) * 3,
        scratch_shapes=[pltpu.SemaphoreType.DMA((3,))],
    )(pltpu.with_memory_space_constraint(raw, pltpu.VMEM))
    return tuple(out[None] for out in outs)


def solution(mesh):
    placed = (P("leaf", "sib", None), P("leaf", "sib", None), P("leaf", None))
    return jax.shard_map(
        on_device,
        mesh=mesh,
        in_specs=placed,
        out_specs=(P("leaf", "sib", None),) * 3,
        check_vma=False,
    )
```

```python
import jax
import jax.numpy as jnp
from jax import lax
from jax.experimental import pallas as pl
from jax.experimental.pallas import tpu as pltpu
from jax.sharding import PartitionSpec as P

MESH = pl.DeviceIdType.MESH
POINTS = 512
ROWS = 64
HALF = 32
BLOCK = 128
PANEL = 2
STRIPS = BLOCK // 8
XR, XL, XO, Y, Z, YC, ZC = 0, 16, 32, 48, 52, 56, 60
COPIES = 64


def matmul(a, b, dims=((1,), (0,))):
    return lax.dot_general(a, b, (dims, ((), ())), preferred_element_type=jnp.float32)


def exact_matmul(a, b):
    return jnp.dot(a, b, precision=lax.Precision.HIGHEST, preferred_element_type=jnp.float32)


def thirds(x):
    high = x.astype(jnp.bfloat16)
    rest = x - high.astype(jnp.float32)
    mid = rest.astype(jnp.bfloat16)
    low = (rest - mid.astype(jnp.float32)).astype(jnp.bfloat16)
    return high, mid, low


def halves(x):
    high = x.astype(jnp.bfloat16)
    return high, (x - high.astype(jnp.float32)).astype(jnp.bfloat16)


def select_rows(onehot, x):
    high, mid, low = thirds(x)
    return matmul(onehot, high) + (matmul(onehot, mid) + matmul(onehot, low))


def select_columns(x, onehot, dims):
    high, mid, low = thirds(x)
    return matmul(high, onehot, dims) + (matmul(mid, onehot, dims) + matmul(low, onehot, dims))


def product(a, b):
    a_high, a_low = halves(a)
    b_high, b_low = halves(b)
    return matmul(a_high, b_high) + (matmul(a_high, b_low) + matmul(a_low, b_high))


def pivot_panel(own, first):
    lane = lax.broadcasted_iota(jnp.int32, (8, BLOCK), 1)
    sub = lax.broadcasted_iota(jnp.int32, (8, BLOCK), 0)
    width = 8 * len(own)
    cols = [[column_of(x, 8 * first + j) for x in own] for j in range(width)]
    pivots = (lane >= 8 * first) & (lane < 8 * first + width)
    s = [jnp.where(pivots, jnp.where(lane - 8 * (first + n) == sub, 1.0, 0.0), x) for n, x in enumerate(own)]
    for j in range(width):
        at, row = divmod(j, 8)
        here = sub == row
        inverse = 1.0 / row_of(cols[j][at], row)
        factor = [jnp.where(here, -1.0, x) if n == at else x for n, x in enumerate(cols[j])]

        def reduced(xs):
            r = row_of(xs[at], row)
            return [(jnp.where(here, 0.0, x) if n == at else x) - (f * r) * inverse for n, (x, f) in enumerate(zip(xs, factor))]

        for q in range(j + 1, width):
            cols[q] = reduced(cols[q])
        s = reduced(s)
    return s, pivots


def row_of(x, j):
    return jnp.broadcast_to(x[j : j + 1, :], (8, BLOCK))


def column_of(x, lane):
    return jnp.broadcast_to(x[:, lane : lane + 1], (8, BLOCK))


def block_inverse(strips):
    strips = list(strips)
    for k in range(0, STRIPS, PANEL):
        s, pivots = pivot_panel(strips[k : k + PANEL], k)
        soon = range(k + PANEL, min(STRIPS, k + 2 * PANEL))
        rest = [i for i in range(STRIPS) if not k <= i < k + PANEL and i not in soon]
        old = list(strips)
        for i in soon:
            t = [column_of(old[i], 8 * k + j) * row_of(s[j // 8], j % 8) for j in range(8 * PANEL)]
            while len(t) > 1:
                t = [t[n] + t[n + 1] for n in range(0, len(t), 2)]
            strips[i] = jnp.where(pivots, 0.0, old[i]) - t[0]
        left = jnp.concatenate([jnp.where(pivots, old[i], 0.0) for i in rest], axis=0)
        zero = jnp.zeros((8, BLOCK), jnp.float32)
        right = jnp.concatenate([s[i - k] if k <= i < k + PANEL else zero for i in range(STRIPS)], axis=0)
        change = exact_matmul(left, right)
        for n, i in enumerate(rest):
            strips[i] = jnp.where(pivots, 0.0, old[i]) - change[8 * n : 8 * n + 8]
        strips[k : k + PANEL] = s
    return jnp.concatenate(strips, axis=0)


def invert(a, panel, between):
    diagonal = [a[pl.ds(8 * i, 8), pl.ds(0, BLOCK)] for i in range(STRIPS)]
    for k in range(POINTS // BLOCK):
        at, after = pl.ds(k * BLOCK, BLOCK), pl.ds((k + 1) * BLOCK, BLOCK)
        inverse = block_inverse(diagonal)
        between[2 * k]()
        if (k + 1) * BLOCK < POINTS:
            ahead = a[after, after] - exact_matmul(a[after, at], exact_matmul(inverse, a[at, after]))
            diagonal = [ahead[8 * i : 8 * i + 8] for i in range(STRIPS)]
        panel[...] = exact_matmul(inverse, a[at, :])
        panel[:, at] = inverse
        a[at, at] = jnp.zeros((BLOCK, BLOCK), jnp.float32)
        column = a[:, at]
        a[:, at] = jnp.zeros((POINTS, BLOCK), jnp.float32)
        a[...] = a[...] - exact_matmul(column, panel[...])
        a[at, :] = panel[...]
        between[2 * k + 1]()


class Exchange:
    def __init__(self, own, view, send_sem, recv_sem, near, has_more):
        self.own, self.view, self.near, self.has_more = own, view, near, has_more
        self.send_sem, self.recv_sem = send_sem, recv_sem

    def copy(self, index, src, dst, to):
        return pltpu.make_async_remote_copy(
            src_ref=src, dst_ref=dst, send_sem=self.send_sem.at[index], recv_sem=self.recv_sem.at[index],
            device_id=self.near[to], device_id_type=MESH,
        )

    def over_y(self, c):
        return self.copy(Y + c, self.own(c), self.view(1, self.near["x"], c), "across_y")

    def over_z(self, c):
        return self.copy(Z + c, self.own(c), self.view(0, self.near["x"], c), "across_z")

    def corner(self, c):
        x = self.near["x"]
        if c % 2:
            return self.copy(YC + c, self.view(2, x, c), self.view(3, x, c), "across_y")
        return self.copy(ZC + c, self.view(1, x, c), self.view(1, x, c), "across_z")

    def to_right(self, kind, c):
        x = self.near["x"]
        src = self.own(c) if kind == 0 else self.view(kind, x, c)
        return self.copy(XR + 4 * kind + c, src, self.view(kind, x, c), "right")

    def to_left(self, kind, c):
        x = self.near["x"]
        src = self.own(c) if kind == 0 else self.view(kind, x, c)
        return self.copy(XL + 4 * kind + c, src, self.view(kind, x, c), "left")

    def to_opposite(self, kind, c):
        x = self.near["x"]
        src = self.own(c) if kind == 0 else self.view(kind, x, c)
        return self.copy(XO + 4 * kind + c, src, self.view(kind, x, c), "opposite")

    def along_x(self, kind, c):
        self.to_right(kind, c).start()
        self.to_left(kind, c).start()
        self.to_opposite(kind, c).start()

    def more(self, kind, run):
        if self.has_more is not None:
            pl.when(self.has_more(kind))(run)

    def first(self):
        def run(even, odd):
            self.over_y(even).start()
            self.over_z(odd).start()
            self.along_x(0, even)
            self.along_x(0, odd)
            self.over_y(odd).start()
            self.over_z(even).start()

        run(0, 1)
        self.more(0, lambda: run(2, 3))

    def second(self):
        def from_y(even, odd):
            self.over_y(even).wait_recv()
            self.corner(even).start()
            self.along_x(1, even)

        def from_z(even, odd):
            self.over_z(odd).wait_recv()
            self.corner(odd).start()
            self.along_x(2, odd)

        def late_y(even, odd):
            self.over_y(odd).wait_recv()
            self.along_x(1, odd)

        def late_z(even, odd):
            self.over_z(even).wait_recv()
            self.along_x(2, even)

        for step in (from_y, from_z, late_y, late_z):
            step(0, 1)

        def more_here():
            from_y(2, 3)
            late_y(2, 3)

        def more_there():
            from_z(2, 3)
            late_z(2, 3)

        self.more(0, more_here)
        self.more(2, more_there)

    def third(self):
        def corners(even, odd):
            self.corner(even).wait_recv()
            self.along_x(3, even)
            self.corner(odd).wait_recv()
            self.along_x(3, odd)

        corners(0, 1)
        self.more(2, lambda: corners(2, 3))

    def last(self, kind):
        def run(even, odd):
            for c in (even, odd):
                self.to_right(kind, c).wait_recv()
                self.to_left(kind, c).wait_recv()
                self.to_opposite(kind, c).wait_recv()

        run(0, 1)
        self.more(kind, lambda: run(2, 3))

    def sent(self):
        def along(kind, even, odd):
            for c in (even, odd):
                self.to_right(kind, c).wait_send()
                self.to_left(kind, c).wait_send()
                self.to_opposite(kind, c).wait_send()

        def across(even, odd):
            for c in (even, odd):
                self.over_y(c).wait_send()
                self.over_z(c).wait_send()

        across(0, 1)
        self.corner(0).wait_send()
        self.corner(1).wait_send()
        for kind in range(4):
            along(kind, 0, 1)

        def more_here():
            across(2, 3)
            self.corner(2).wait_send()
            along(0, 2, 3)
            along(1, 2, 3)

        def more_there():
            self.corner(3).wait_send()
            along(2, 2, 3)
            along(3, 2, 3)

        self.more(0, more_here)
        self.more(2, more_there)


def place_rows(tiles, matrix, box, half):
    rows = pl.ds(pl.multiple_of(half * 4 * ROWS, 4 * ROWS), 4 * ROWS)
    matrix[rows, :] = jnp.zeros((4 * ROWS, POINTS), jnp.float32)
    for x in range(4):
        block = box * 8 + half * 4 + x
        tile = 2 * half + x // 2
        at = pl.ds(pl.multiple_of((half * 4 + x) * ROWS, ROWS), ROWS)
        for t in range(3):
            lanes = pl.ds(pl.multiple_of((tile + t) % 4 * BLOCK, BLOCK), BLOCK)
            matrix[at, lanes] = tiles[block, t] * (0.5 if t == 0 else 1.0)
    return rows


def kernel(t_ref, map_ref, ext_ref, raw_ref, tiles, outer, other_map, near_part, far_part, shuffle, a, panel, send_sem, recv_sem, map_sem, keep_sem):
    sib, leaf = lax.axis_index("sib"), lax.axis_index("leaf")
    leaves = lax.axis_size("leaf")
    x, z = sib % 4, sib // 4
    near = {
        "x": x, "z": z,
        "right": {"sib": z * 4 + (x + 1) % 4},
        "left": {"sib": z * 4 + (x + 3) % 4},
        "opposite": {"sib": z * 4 + (x + 2) % 4},
        "across_z": {"sib": (sib + 4) % 8},
        "across_y": {"leaf": (leaf + leaves // 2) % leaves},
    }
    barrier = pltpu.get_barrier_semaphore()
    for name in ("right", "left", "opposite", "across_z", "across_y"):
        pl.semaphore_signal(barrier, inc=1, device_id=near[name], device_id_type=MESH)
    pl.semaphore_wait(barrier, 5)

    map_copy = pltpu.make_async_remote_copy(
        src_ref=map_ref, dst_ref=other_map, send_sem=map_sem.at[0], recv_sem=map_sem.at[1],
        device_id=near["across_y"], device_id_type=MESH,
    )
    map_copy.start()

    def z_of(kind):
        return z if kind < 2 else 1 - z

    def own_tile(c):
        lanes = pl.ds(pl.multiple_of(POINTS + (sib // 2 + min(c, 2)) % 4 * BLOCK, BLOCK), BLOCK)
        return t_ref.at[:, lanes] if c < 2 else t_ref.at[pl.ds((c - 2) * HALF, HALF), lanes]

    def tile_view(kind, x, c):
        block = tiles.at[kind % 2 * 8 + z_of(kind) * 4 + x, min(c, 2)]
        return block if c < 2 else block.at[pl.ds((c - 2) * HALF, HALF), :]

    def own_rows(c):
        return t_ref.at[pl.ds(c * HALF, HALF), pl.ds(0, POINTS)]

    def row_view(kind, x, c):
        return outer.at[pl.ds(kind % 2 * POINTS + (z_of(kind) * 4 + x) * ROWS + c * HALF, HALF), :]

    g = Exchange(own_tile, tile_view, send_sem.at[0], recv_sem.at[0], near, lambda kind: z_of(kind) == 0)
    r = Exchange(own_rows, row_view, send_sem.at[1], recv_sem.at[1], near, None)
    g.first()

    def keep(n):
        if n == 3:
            mine = pl.ds(pl.multiple_of(sib * ROWS, ROWS), ROWS)
            return pltpu.make_async_copy(t_ref.at[:, pl.ds(0, POINTS)], outer.at[mine, :], keep_sem.at[n])
        lanes = pl.ds(pl.multiple_of(POINTS + (sib // 2 + n) % 4 * BLOCK, BLOCK), BLOCK)
        return pltpu.make_async_copy(t_ref.at[:, lanes], tiles.at[sib, n], keep_sem.at[n])

    for n in (0, 1, 3):
        keep(n).start()
    ext_copy = pltpu.make_async_copy(ext_ref, raw_ref.at[pl.ds(0, ROWS), :], keep_sem.at[4])
    ext_copy.start()
    pl.when(z == 0)(lambda: keep(2).start())

    for block in (4, 5, 6, 7, 12, 13, 14, 15):
        tiles[block, 2] = jnp.zeros((ROWS, BLOCK), jnp.float32)
    g.second()
    map_copy.wait()
    point = lax.broadcasted_iota(jnp.int32, (POINTS, POINTS), 0)
    own_onehot = jnp.where(point == map_ref[...], 1.0, 0.0).astype(jnp.bfloat16)
    other_onehot = jnp.where(point == other_map[...], 1.0, 0.0).astype(jnp.bfloat16)
    shuffle[...] = matmul(own_onehot, other_onehot, ((0,), (0,))).astype(jnp.bfloat16)
    g.third()
    r.first()
    for n in (0, 1, 3):
        keep(n).wait()
    ext_copy.wait()
    pl.when(z == 0)(lambda: keep(2).wait())

    def permuted(half):
        rows = place_rows(tiles, far_part, 1, half)
        moved = select_columns(far_part[rows, :], shuffle[...], ((1,), (1,)))
        lanes = pl.ds(pl.multiple_of(half * 4 * ROWS, 4 * ROWS), 4 * ROWS)
        return select_rows(shuffle[:, lanes], moved)

    g.last(1)
    near_part[...] = permuted(z)
    g.last(0)
    place_rows(tiles, a, 0, z)
    g.last(2)
    place_rows(tiles, a, 0, 1 - z)
    g.last(3)
    near_part[...] = (near_part[...] + a[...]) + permuted(1 - z)
    for i in range(4):
        for j in range(4):
            rows, lanes = pl.ds(i * BLOCK, BLOCK), pl.ds(j * BLOCK, BLOCK)
            a[rows, lanes] = near_part[rows, lanes] + near_part[lanes, rows].T

    def nothing():
        pass

    invert(a, panel, (r.second, nothing, nothing, nothing, r.third, nothing, nothing, nothing))

    rows = lax.broadcasted_iota(jnp.int32, (ROWS, POINTS), 0) + sib * ROWS
    chosen = select_rows(jnp.where(rows == map_ref[...], 1.0, 0.0).astype(jnp.bfloat16), a[...])
    r.last(0)
    r.last(2)
    wide = outer[pl.ds(0, POINTS), pl.ds(pl.multiple_of(sib // 2 * BLOCK, BLOCK), BLOCK)]
    wide = pltpu.roll(wide, (sib % 2) * ROWS, 1)[:, :ROWS]
    right = product(wide.T, a[...])
    both = product(jnp.concatenate([right, chosen], axis=0), outer[pl.ds(0, POINTS), :])
    raw_ref[:ROWS] = raw_ref[:ROWS] - both[:ROWS]
    raw_ref[2 * ROWS :] = -both[ROWS:]
    moved = select_columns(right, shuffle[...], ((1,), (0,)))
    r.last(1)
    r.last(3)
    raw_ref[ROWS : 2 * ROWS] = -product(moved, outer[pl.ds(POINTS, POINTS), :])
    g.sent()
    r.sent()


def outputs(raw_ref, own_ref, cross_ref, sol_ref, sem):
    copies = [
        pltpu.make_async_copy(raw_ref.at[pl.ds(n * ROWS, ROWS), :], out, sem.at[n])
        for n, out in enumerate((own_ref, cross_ref, sol_ref))
    ]
    for copy in copies:
        copy.start()
    for copy in copies:
        copy.wait()


def on_device(t_int, t_ext, iface_map):
    vmem = pl.BlockSpec(memory_space=pltpu.VMEM)
    anywhere = pl.BlockSpec(memory_space=pl.ANY)
    raw = pl.pallas_call(
        kernel,
        out_shape=pltpu.VMEM((3 * ROWS, POINTS), jnp.float32),
        in_specs=[anywhere, vmem, anywhere],
        out_specs=vmem,
        scratch_shapes=[
            pltpu.VMEM((16, 3, ROWS, BLOCK), jnp.float32),
            pltpu.VMEM((2 * POINTS, POINTS), jnp.float32),
            pltpu.VMEM((1, POINTS), jnp.int32),
            pltpu.VMEM((POINTS, POINTS), jnp.float32),
            pltpu.VMEM((POINTS, POINTS), jnp.float32),
            pltpu.VMEM((POINTS, POINTS), jnp.bfloat16),
            pltpu.VMEM((POINTS, POINTS), jnp.float32),
            pltpu.VMEM((BLOCK, POINTS), jnp.float32),
            pltpu.SemaphoreType.DMA((2, COPIES)),
            pltpu.SemaphoreType.DMA((2, COPIES)),
            pltpu.SemaphoreType.DMA((2,)),
            pltpu.SemaphoreType.DMA((5,)),
        ],
        compiler_params=pltpu.CompilerParams(collective_id=0, has_side_effects=True),
    )(t_int[0], iface_map, t_ext[0])
    block = jax.ShapeDtypeStruct((ROWS, POINTS), jnp.float32)
    outs = pl.pallas_call(
        outputs,
        out_shape=(block,) * 3,
        in_specs=[vmem],
        out_specs=(anywhere,) * 3,
        scratch_shapes=[pltpu.SemaphoreType.DMA((3,))],
    )(pltpu.with_memory_space_constraint(raw, pltpu.VMEM))
    return tuple(out[None] for out in outs)


def solution(mesh):
    placed = (P("leaf", "sib", None), P("leaf", "sib", None), P("leaf", None))
    return jax.shard_map(
        on_device,
        mesh=mesh,
        in_specs=placed,
        out_specs=(P("leaf", "sib", None),) * 3,
        check_vma=False,
    )
```
